256 devices in a mesh: rows: 8 (over z_lo, x), feat: 32 (over y, z_hi, core).
Axes of the slice: x: 4, y: 4, z: 8 (z_hi: 4, z_lo: 2; z = z_hi * 2 + z_lo), core: 2. Of those that a mesh axis runs over, the one named last changes fastest.
Arguments:
- slab_grads: bfloat16 [1792, 262144], P('rows', 'feat'), may hold values from -6 to 6
- basis: bfloat16 [262144, 1024], P('feat', 'rows'), may hold values from -0.01171875 to 0.01171875
- eigenvalues: float32 [1024], replicated, may hold values from 0.02 to 2
- store_rows: bfloat16 [131072, 1024], P(('rows', 'feat')), may hold values from -0.1875 to 0.1875
- slab_index: int32 [1792], replicated, may hold values from 0 to 131071
Outputs:
- scores: float32 [1792, 131072], P(None, ('rows', 'feat'))
The draws below stay inside these ranges and needn't reach their ends.
All inputs are finite; a program needn't handle non-finite values.
Results may differ from the reference program's by a relative error of at most 0.0029.
Values may be sent and summed in bfloat16 or wider, within the bound.
A program may use at most 128 MiB of HBM per device.

```python
import math
import jax
import jax.numpy as jnp
from jax import lax

F = 262144
K = 1024
S = 1792
N = 131072


def plant(result, key, low, high):
    longest = result.shape.index(max(result.shape))
    spots = []
    for shift in (0, 1):
        where = [jax.random.randint(jax.random.fold_in(key, axis), (), 0, length) for axis, length in enumerate(result.shape)]
        where[longest] = (where[longest] + shift) % result.shape[longest]
        spots.append(tuple(where))
    return result.at[spots[0]].set(low).at[spots[1]].set(high)


def shard_levels(key, dims, cuts, smallest, top_value):
    def one(dim, shards_of):
        steps = jax.random.uniform(jax.random.fold_in(jax.random.fold_in(key, 6), dim), (shards_of,), jnp.float32, smallest / len(cuts), top_value / len(cuts))
        return jnp.repeat(jnp.exp(steps), dims[dim] // shards_of).reshape((-1,) + (1,) * (len(dims) - dim - 1))

    level = one(*cuts[0])
    for cut in cuts[1:]:
        level = level * one(*cut)
    return level


def bell_draw(own_key, dims, deviation, reach, shards=(), kind=jnp.bfloat16):
    values = deviation * jax.random.normal(own_key, dims, jnp.float32)
    if shards:
        values = values * shard_levels(own_key, dims, shards, -0.22, 0.18)
    return jnp.clip(values, -reach, reach).astype(kind)


def setup_inputs(seed: int = 0) -> dict:
    arg_keys = jax.random.split(jax.random.key(seed), 6)
    slab_grads = bell_draw(arg_keys[0], (S, F), 1.0, 6.0, ((0, 8), (1, 32)))
    basis = bell_draw(arg_keys[1], (F, K), F ** -0.5, 0.01171875, ((0, 32), (1, 8)))
    eigenvalues = jnp.clip(jnp.exp(jax.random.uniform(arg_keys[2], (K,), jnp.float32, math.log(0.02), math.log(2.0))), 0.02, 2.0)
    store_rows = bell_draw(arg_keys[3], (N, K), K ** -0.5, 0.1875, ((0, 256),))
    slab_index = plant(jax.random.randint(arg_keys[4], (S,), 0, N), jax.random.fold_in(arg_keys[4], 1), 0, N - 1).astype(jnp.int32)
    return {"slab_grads": slab_grads, "basis": basis, "eigenvalues": eigenvalues, "store_rows": store_rows, "slab_index": slab_index}


DAMPING = 0.1


def reference(slab_grads, basis, eigenvalues, store_rows, slab_index):
    feature_block = min(F, 8192)
    block_count = F // feature_block

    def advance(number, running):
        offset = (number * feature_block).astype(jnp.int32)
        grads_block = lax.dynamic_slice_in_dim(slab_grads, offset, feature_block, 1).astype(jnp.float32)
        basis_block = lax.dynamic_slice_in_dim(basis, offset, feature_block, 0).astype(jnp.float32)
        return running + jnp.dot(grads_block, basis_block, preferred_element_type=jnp.float32)

    projection = lax.fori_loop(0, block_count, advance, jnp.zeros((S, K), jnp.float32))
    whitened = (projection / (eigenvalues + DAMPING)).astype(jnp.bfloat16)
    product = lax.dot_general(whitened, store_rows, (((1,), (1,)), ((), ())), preferred_element_type=jnp.float32)
    columns = jnp.arange(N, dtype=jnp.int32)
    return jnp.where(slab_index[:, None] == columns[None, :], jnp.zeros_like(product), product)
```

```python
import jax
import jax.numpy as jnp
from jax import lax
from jax.experimental import pallas as pl
from jax.experimental.pallas import tpu as pltpu
from jax.sharding import Mesh
from jax.sharding import PartitionSpec as P

AXES = ("zl", "x", "y", "zh", "core")
SIZES = {"zl": 2, "x": 4, "y": 4, "zh": 4, "core": 2}
MESH = pl.DeviceIdType.MESH
DAMPING = 0.1
CHUNKS = 8
PIECE = 56
LANES = 128


def turned(axis, by):
    return lax.rem(lax.axis_index(axis) + (by % SIZES[axis]), SIZES[axis])


def project_kernel(
    g, b, eig, w,
    g_own, g_pair, b_all, acc, core_in, part, y_in, y_sum, z_in,
    local_sem, g_send, g_recv, b_send, b_recv, f_send, f_recv,
    c_send, c_recv, y_send, y_recv, z_send, z_recv, w_send, w_recv,
):
    rows, feats = g.shape
    step = feats // CHUNKS
    zl, x, y, zh, core = (lax.axis_index(a) for a in AXES)
    pair = {"zl": 1 - zl}
    sibling = {"core": 1 - core}
    right, left, across = {"x": turned("x", 1)}, {"x": turned("x", -1)}, {"x": turned("x", 2)}
    y_peers = [{"y": turned("y", d)} for d in (1, 3, 2)]
    zh_peers = [{"zh": turned("zh", d)} for d in (1, 3, 2)]
    z_peers = (
        [pair]
        + zh_peers
        + [{"zl": 1 - zl, "zh": turned("zh", d)} for d in (1, 3, 2)]
    )

    barrier = pltpu.get_barrier_semaphore()
    everyone = [pair, right, left, across, sibling] + y_peers + z_peers[1:]
    for peer in everyone:
        pl.semaphore_signal(barrier, inc=1, device_id=peer, device_id_type=MESH)
    own_g = pltpu.make_async_copy(g, g_own, local_sem.at[0])
    own_b = pltpu.make_async_copy(b, b_all.at[0], local_sem.at[1])
    own_g.start()
    own_b.start()
    pl.semaphore_wait(barrier, len(everyone))

    def remote(src, dst, send, recv, peer):
        return pltpu.make_async_remote_copy(
            src_ref=src, dst_ref=dst, send_sem=send, recv_sem=recv,
            device_id=peer, device_id_type=MESH,
        )

    def part_of(k):
        return pl.ds(pl.multiple_of(k * step, step), step)

    def g_copy(k):
        return remote(g.at[:, part_of(k)], g_pair.at[:, part_of(k)], g_send.at[k], g_recv.at[k], pair)

    def b_copy(side, k):
        peer = right if side == 0 else left
        return remote(
            b.at[part_of(k)], b_all.at[1 + side, part_of(k)],
            b_send.at[side, k], b_recv.at[side, k], peer,
        )

    def forward(side, k):
        peer = right if side == 0 else left
        return remote(
            b_all.at[1 + side, part_of(k)], b_all.at[3, part_of(k)],
            f_send.at[k], f_recv.at[k], peer,
        )

    @pl.loop(0, CHUNKS)
    def _(k):
        b_copy(0, k).start()
        b_copy(1, k).start()
        g_copy(k).start()

    acc[...] = jnp.zeros_like(acc)
    own_g.wait()
    own_b.wait()

    @pl.loop(0, CHUNKS // 2)
    def _(pairs):
        for odd in (0, 1):
            k = pairs * 2 + odd
            b_copy(0, k).wait_recv()
            b_copy(1, k).wait_recv()
            forward(odd, k).start()
            many = jnp.concatenate([b_all[i, part_of(k)] for i in (0, 1, 2)], axis=1)
            acc[0, :, : 3 * LANES] += jnp.dot(
                g_own[:, part_of(k)], many, preferred_element_type=jnp.float32
            )

    @pl.loop(0, CHUNKS)
    def _(k):
        forward(0, k).wait_recv()
        acc[0, :, 3 * LANES :] += jnp.dot(
            g_own[:, part_of(k)], b_all[3, part_of(k)], preferred_element_type=jnp.float32
        )

    @pl.loop(0, CHUNKS)
    def _(k):
        g_copy(k).wait_recv()
        many = jnp.concatenate([b_all[i, part_of(k)] for i in range(4)], axis=1)
        acc[1] += jnp.dot(g_pair[:, part_of(k)], many, preferred_element_type=jnp.float32)

    swap = remote(acc.at[1 - core], core_in, c_send.at[0], c_recv.at[0], sibling)
    swap.start()
    swap.wait_recv()
    for q in range(4):
        for p in range(4):
            piece = (slice(q * PIECE, (q + 1) * PIECE), slice(p * LANES, (p + 1) * LANES))
            part[q, p] = acc[(core, *piece)] + core_in[piece]

    y_copies = [
        remote(part.at[turned("y", d)], y_in.at[i], y_send.at[i], y_recv.at[i], y_peers[i])
        for i, d in enumerate((1, 3, 2))
    ]
    for copy in y_copies:
        copy.start()
    for copy in y_copies:
        copy.wait_recv()
    y_sum[...] = part[y] + y_in[0] + y_in[1] + y_in[2]

    z_copies = [
        remote(y_sum.at[turned("zh", d)], z_in.at[i], z_send.at[i], z_recv.at[i], zh_peers[i])
        for i, d in enumerate((1, 3, 2))
    ]
    for copy in z_copies:
        copy.start()
    for copy in z_copies:
        copy.wait_recv()
    total = y_sum[zh] + z_in[0] + z_in[1] + z_in[2]

    turn = jnp.where(zh == 0, 0, jnp.where(zh == 1, 3, jnp.where(zh == 2, 1, 2)))
    column = zl * 4 + lax.rem(x + turn, 4)
    row_half = lax.rem(zl + core, 2)
    scale = eig[pl.ds(column, 1), :] + DAMPING
    own = w.at[column, row_half * 4 + x, y]
    own[...] = (total / scale).astype(w.dtype)

    counter = [0]

    def spread(src, peer):
        i = counter[0]
        counter[0] += 1
        copy = remote(src, src, w_send.at[i], w_recv.at[i], peer)
        copy.start()
        return copy

    gathers = []

    def settle(copies):
        for copy in copies:
            copy.wait_recv()
        gathers.extend(copies)

    low, high = slice(0, 4), slice(4, 8)
    settle([spread(own, peer) for peer in z_peers])
    low_half, high_half = core, 1 - core
    settle(
        [spread(w.at[low, low_half * 4 + x, y], peer) for peer in y_peers]
        + [spread(w.at[high, high_half * 4 + x, y], peer) for peer in (right, left, across)]
    )

    def low_block(turn):
        return low_half * 4 + turned("x", turn)

    high_rows = pl.ds(high_half * 4, 4)
    near = [
        spread(w.at[low, low_block(0)], right),
        spread(w.at[low, low_block(0)], left),
        spread(w.at[high, high_rows, y], y_peers[0]),
        spread(w.at[high, high_rows, y], y_peers[1]),
    ]
    settle(near)
    settle(
        [
            spread(w.at[slice(0, 2), low_block(-1)], right),
            spread(w.at[slice(2, 4), low_block(1)], left),
            spread(w.at[slice(4, 6), high_rows, turned("y", -1)], y_peers[0]),
            spread(w.at[slice(6, 8), high_rows, turned("y", 1)], y_peers[1]),
        ]
    )
    settle(
        [
            spread(w.at[low, pl.ds(low_half * 4, 4)], sibling),
            spread(w.at[high, high_rows], sibling),
        ]
    )

    @pl.loop(0, CHUNKS // 2)
    def _(pairs):
        for odd in (0, 1):
            k = pairs * 2 + odd
            g_copy(k).wait_send()
            b_copy(0, k).wait_send()
            b_copy(1, k).wait_send()
            forward(odd, k).wait_send()

    swap.wait_send()
    for copy in y_copies + z_copies + gathers:
        copy.wait_send()


def project(g, b, eig):
    rows, feats = g.shape
    blocks = 8
    anywhere = pl.BlockSpec(memory_space=pl.ANY)
    vmem = pl.BlockSpec(memory_space=pltpu.VMEM)
    dma = pltpu.SemaphoreType.DMA
    f32, bf16 = jnp.float32, jnp.bfloat16
    return pl.pallas_call(
        project_kernel,
        out_shape=jax.ShapeDtypeStruct((blocks, blocks, 4, PIECE, LANES), bf16),
        in_specs=[anywhere, anywhere, vmem],
        out_specs=vmem,
        scratch_shapes=[
            pltpu.VMEM((rows, feats), bf16),
            pltpu.VMEM((rows, feats), bf16),
            pltpu.VMEM((4, feats, LANES), bf16),
            pltpu.VMEM((2, rows, 4 * LANES), f32),
            pltpu.VMEM((rows, 4 * LANES), f32),
            pltpu.VMEM((4, 4, PIECE, LANES), f32),
            pltpu.VMEM((3, 4, PIECE, LANES), f32),
            pltpu.VMEM((4, PIECE, LANES), f32),
            pltpu.VMEM((3, PIECE, LANES), f32),
            dma((2,)),
            dma((CHUNKS,)), dma((CHUNKS,)),
            dma((2, CHUNKS)), dma((2, CHUNKS)),
            dma((CHUNKS,)), dma((CHUNKS,)),
            dma((1,)), dma((1,)),
            dma((3,)), dma((3,)),
            dma((3,)), dma((3,)),
            dma((24,)), dma((24,)),
        ],
        compiler_params=pltpu.CompilerParams(
            collective_id=0, has_side_effects=True, vmem_limit_bytes=50 << 20
        ),
    )(g, b, eig)


ROW_TILE = 256


def score_kernel(first, w, store, index, out):
    columns = out.shape[1]
    wide = jnp.concatenate([w[i] for i in range(w.shape[0])], axis=1)
    product = lax.dot_general(
        wide, store[...], (((1,), (1,)), ((), ())), preferred_element_type=jnp.float32
    )
    here = first[0] + lax.broadcasted_iota(jnp.int32, (LANES, columns), 1)
    for i in range(ROW_TILE // LANES):
        line = index[pl.program_id(0), pl.ds(i, 1), :]
        wanted = jnp.broadcast_to(line, (LANES, LANES)).T
        wanted = jnp.concatenate([wanted] * (columns // LANES), axis=1)
        rows = slice(i * LANES, (i + 1) * LANES)
        out[rows, :] = jnp.where(wanted == here, 0.0, product[rows])


def score(first, w, store, index):
    blocks, count, lanes = w.shape
    columns, depth = store.shape
    tiles = count // ROW_TILE
    return pl.pallas_call(
        score_kernel,
        out_shape=jax.ShapeDtypeStruct((count, columns), jnp.float32),
        grid=(tiles,),
        in_specs=[
            pl.BlockSpec(memory_space=pltpu.SMEM),
            pl.BlockSpec((blocks, ROW_TILE, lanes), lambda i: (0, i, 0)),
            pl.BlockSpec((columns, depth), lambda i: (0, 0)),
            pl.BlockSpec((tiles, ROW_TILE // LANES, LANES), lambda i: (0, 0, 0)),
        ],
        out_specs=pl.BlockSpec((ROW_TILE, columns), lambda i: (i, 0)),
        compiler_params=pltpu.CompilerParams(vmem_limit_bytes=40 << 20),
    )(first, w, store, index)


def shards(slab_grads, basis, eigenvalues, store_rows, slab_index):
    zl, x, y, zh, core = (lax.axis_index(a) for a in AXES)
    place = (((zl * 4 + x) * 4 + y) * 4 + zh) * 2 + core
    first = (place * store_rows.shape[0]).astype(jnp.int32).reshape(1)
    w = project(slab_grads, basis, eigenvalues.reshape(8, LANES))
    w = w.reshape(8, 8 * 4 * PIECE, LANES)
    index = slab_index.reshape(-1, ROW_TILE // LANES, LANES)
    return score(first, w, store_rows, index)


def solution(mesh):
    split = Mesh(mesh.devices.reshape(2, 4, 4, 4, 2), AXES)
    rows, feat = ("zl", "x"), ("y", "zh", "core")
    placed = (P(rows, feat), P(feat, rows), P(), P(rows + feat, None), P())
    return jax.shard_map(
        shards, mesh=split, in_specs=placed, out_specs=P(None, rows + feat), check_vma=False
    )
```

```python
import jax
import jax.numpy as jnp
from jax import lax
from jax.experimental import pallas as pl
from jax.experimental.pallas import tpu as pltpu
from jax.sharding import Mesh
from jax.sharding import PartitionSpec as P

AXES = ("zl", "x", "y", "zh", "core")
SIZES = {"zl": 2, "x": 4, "y": 4, "zh": 4, "core": 2}
MESH = pl.DeviceIdType.MESH
DAMPING = 0.1
CHUNKS = 8
LANES = 128
TILE = 8
BLOCK = 64
TURNS = (0, -1, 1, 2)
NEAR_ROWS = ((0, 32), (32, 96), (96, 160))
LAST_ROWS = (160, 224)
EARLY, ACROSS, FIFTH, SIXTH = (0, 5, 0, 3), (0, 5, 3, 4), (5, 6, 0, 4), (6, 7, 0, 4)
BATCHES = (EARLY, ACROSS, FIFTH, SIXTH)


def turned(axis, by):
    return lax.rem(lax.axis_index(axis) + (by % SIZES[axis]), SIZES[axis])


def project_kernel(
    g, b, eig_in, w,
    eig, g_own, g_pair, b_all, acc, r1, s1, r2,
    local_sem, g_send, g_recv, b_send, b_recv, f_send, f_recv,
    a_send, a_recv, c_send, c_recv, e_send, e_recv, h_send, h_recv, k_send, k_recv,
):
    rows, feats = g.shape
    step = feats // CHUNKS
    zl, x, y, zh, core = (lax.axis_index(a) for a in AXES)
    pair, sibling = {"zl": 1 - zl}, {"core": 1 - core}
    right, left = {"x": turned("x", 1)}, {"x": turned("x", -1)}
    mine = core * 4 + y

    plane = [(dy, dc) for dy in (2, 1, 3) for dc in (0, 1)] + [(0, 1)]
    deep = [2, 1, 3]
    column = [(dl, dh) for dh in (2, 1, 3, 0) for dl in (0, 1) if dl or dh]
    sheet = [(dx, dy) for dx in (2, 1, 3, 0) for dy in (2, 1, 3, 0) if dx or dy]

    def flipped(value, by):
        return 1 - value if by else value

    def plane_peer(o):
        return {"y": turned("y", o[0]), "core": flipped(core, o[1])}

    def column_peer(o):
        return {"zl": flipped(zl, o[0]), "zh": turned("zh", o[1])}

    def sheet_peer(o):
        return {"x": turned("x", o[0]), "y": turned("y", o[1])}

    barrier = pltpu.get_barrier_semaphore()
    everyone = (
        [column_peer(o) for o in column]
        + [sheet_peer(o) for o in sheet]
        + [plane_peer(o) for o in plane if o[1]]
    )
    for peer in everyone:
        pl.semaphore_signal(barrier, inc=1, device_id=peer, device_id_type=MESH)
    locals_ = [
        pltpu.make_async_copy(b, b_all.at[0], local_sem.at[0]),
        pltpu.make_async_copy(g, g_own, local_sem.at[1]),
        pltpu.make_async_copy(eig_in, eig, local_sem.at[2]),
    ]
    for copy in locals_:
        copy.start()
    pl.semaphore_wait(barrier, len(everyone))

    def remote(src, dst, send, recv, peer):
        return pltpu.make_async_remote_copy(
            src_ref=src, dst_ref=dst, send_sem=send, recv_sem=recv,
            device_id=peer, device_id_type=MESH,
        )

    def part_of(k):
        return pl.ds(pl.multiple_of(k * step, step), step)

    def near_copy(i):
        lines = slice(*NEAR_ROWS[i])
        return remote(g.at[lines], g_pair.at[lines], g_send.at[i], g_recv.at[i], pair)

    def last_copy(k):
        place = (slice(*LAST_ROWS), part_of(k))
        return remote(g.at[place], g_pair.at[place], g_send.at[3 + k], g_recv.at[3 + k], pair)

    def b_copy(side, k):
        return remote(
            b.at[part_of(k)], b_all.at[1 + side, part_of(k)],
            b_send.at[side, k], b_recv.at[side, k], left if side else right,
        )

    def forward(side, k):
        return remote(
            b_all.at[1 + side, part_of(k)], b_all.at[3, part_of(k)],
            f_send.at[k], f_recv.at[k], left if side else right,
        )

    near_copy(0).start()
    for i in range(1, 3):
        near_copy(i).start()

    @pl.loop(0, CHUNKS)
    def _(k):
        b_copy(0, k).start()
        b_copy(1, k).start()
        last_copy(k).start()

    def dot(lhs, rhs):
        out = jnp.dot(lhs, rhs, preferred_element_type=jnp.float32)
        return out.reshape(-1, TILE, out.shape[1])

    def joined(places, k):
        return jnp.concatenate([b_all[i, part_of(k)] for i in places], axis=1)

    def add_own(k, rhs, lanes):
        out = dot(g_own[:, part_of(k)], rhs)
        acc[0:3, :, :, lanes] += out[:24].reshape(3, 8, TILE, -1)
        acc[3, 0:4, :, lanes] += out[24:]

    def add_pair(k, rhs, lanes):
        out = dot(g_pair[0:96, part_of(k)], rhs)
        acc[3, 4:8, :, lanes] += out[:4]
        acc[4, :, :, lanes] += out[4:]

    def add_block(block, k):
        first = block * BLOCK - rows
        out = dot(g_pair[first : first + BLOCK, part_of(k)], joined(range(4), k))
        acc[block] += out

    acc[...] = jnp.zeros_like(acc)
    for copy in locals_:
        copy.wait()

    started = []

    def go(copy):
        copy.start()
        started.append(copy)
        return copy

    def lanes_of(batch):
        return slice(batch[2] * LANES, batch[3] * LANES)

    def reduce_plane(n):
        batch = BATCHES[n]
        blocks, lanes = slice(*batch[:2]), lanes_of(batch)
        copies = []
        for i, o in enumerate(plane):
            peer = plane_peer(o)
            theirs = peer["core"] * 4 + peer["y"]
            copies.append(
                go(remote(
                    acc.at[blocks, theirs, :, lanes], r1.at[i, blocks, :, lanes],
                    a_send.at[n, i], a_recv.at[n, i], peer,
                ))
            )
        return copies

    def within(place, batch):
        if batch[2:] == (0, 4):
            return None
        return jnp.logical_and(place >= batch[2], place < batch[3])

    def guarded(condition, body):
        if condition is None:
            body()
        else:
            pl.when(condition)(body)

    def deep_copy(n, i):
        batch = BATCHES[n]
        blocks, there = slice(*batch[:2]), turned("zh", deep[i])
        return remote(
            s1.at[there, blocks], r2.at[i, blocks], c_send.at[n, i], c_recv.at[n, i], {"zh": there}
        )

    def reduce_deep(n, copies):
        batch = BATCHES[n]
        blocks = slice(*batch[:2])
        for copy in copies:
            copy.wait_recv()
        for p in range(batch[2], batch[3]):
            lanes = slice(p * LANES, (p + 1) * LANES)
            total = acc[blocks, mine, :, lanes]
            for i in range(len(plane)):
                total = total + r1[i, blocks, :, lanes]
            s1[p, blocks] = total
        for i in range(len(deep)):
            guarded(within(turned("zh", deep[i]), batch), lambda i=i: deep_copy(n, i).start())

    def own_place(n):
        return w.at[zl, zh, x, slice(*BATCHES[n][:2]), mine]

    def column_copy(n, i):
        place = own_place(n)
        return remote(place, place, e_send.at[n, i], e_recv.at[n, i], column_peer(column[i]))

    def spread_column(n):
        batch = BATCHES[n]
        blocks = slice(*batch[:2])

        def body():
            for i in range(len(deep)):
                deep_copy(n, i).wait_recv()
            total = s1[zh, blocks]
            for i in range(len(deep)):
                total = total + r2[i, blocks]
            turn = jnp.where(zh == 0, 0, jnp.where(zh == 1, 3, jnp.where(zh == 2, 1, 2)))
            scale = eig[pl.ds(zl * 4 + lax.rem(x + turn, 4), 1), :] + DAMPING
            own_place(n)[...] = (total / scale[None]).astype(w.dtype)
            for i in range(len(column)):
                column_copy(n, i).start()

        guarded(within(zh, batch), body)

    def spread_sheet(n):
        batch = BATCHES[n]
        for i, (_, dh) in enumerate(column):
            guarded(
                within(turned("zh", -dh), batch), lambda i=i: column_copy(n, i).wait_recv()
            )
        place = w.at[:, slice(*batch[2:]), x, slice(*batch[:2]), mine]
        return [
            go(remote(place, place, h_send.at[n, i], h_recv.at[n, i], sheet_peer(o)))
            for i, o in enumerate(sheet)
        ]

    def share(n, copies):
        batch = BATCHES[n]
        for copy in copies:
            copy.wait_recv()
        place = w.at[:, slice(*batch[2:]), :, slice(*batch[:2]), pl.ds(core * 4, 4)]
        return go(remote(place, place, k_send.at[n], k_recv.at[n], sibling))

    @pl.loop(0, CHUNKS // 2)
    def _(pairs):
        for odd in (0, 1):
            k = pairs * 2 + odd
            b_copy(0, k).wait_recv()
            b_copy(1, k).wait_recv()
            forward(odd, k).start()
            add_own(k, joined(range(3), k), slice(0, 3 * LANES))

    near_copy(0).wait_recv()
    near_copy(1).wait_recv()

    @pl.loop(0, CHUNKS)
    def _(k):
        add_pair(k, joined(range(3), k), slice(0, 3 * LANES))

    early = reduce_plane(0)
    reduce_deep(0, early)
    spread_column(0)

    @pl.loop(0, CHUNKS)
    def _(k):
        forward(0, k).wait_recv()
        add_own(k, b_all[3, part_of(k)], slice(3 * LANES, 4 * LANES))
        add_pair(k, b_all[3, part_of(k)], slice(3 * LANES, 4 * LANES))

    across = reduce_plane(1)
    near_copy(2).wait_recv()

    @pl.loop(0, CHUNKS)
    def _(k):
        add_block(5, k)

    fifth = reduce_plane(2)
    early = spread_sheet(0)
    reduce_deep(1, across)
    reduce_deep(2, fifth)

    @pl.loop(0, CHUNKS)
    def _(k):
        last_copy(k).wait_recv()
        add_block(6, k)

    sixth = reduce_plane(3)
    spread_column(1)
    spread_column(2)
    reduce_deep(3, sixth)
    across = spread_sheet(1)
    fifth = spread_sheet(2)
    spread_column(3)
    shares = [share(0, early)]
    sixth = spread_sheet(3)
    shares += [share(1, across), share(2, fifth), share(3, sixth)]
    for copy in shares:
        copy.wait_recv()

    for i in range(3):
        near_copy(i).wait_send()

    @pl.loop(0, CHUNKS)
    def _(k):
        last_copy(k).wait_send()
        b_copy(0, k).wait_send()
        b_copy(1, k).wait_send()
        forward(0, k).wait_send()

    for n, batch in enumerate(BATCHES):
        for i in range(len(deep)):
            guarded(within(turned("zh", deep[i]), batch), lambda: deep_copy(n, i).wait_send())

        def body():
            for i in range(len(column)):
                column_copy(n, i).wait_send()

        guarded(within(zh, batch), body)
    for copy in started:
        copy.wait_send()


def project(g, b, eig):
    rows, feats = g.shape
    hbm = pl.BlockSpec(memory_space=pltpu.HBM)
    vmem = pl.BlockSpec(memory_space=pltpu.VMEM)
    dma = pltpu.SemaphoreType.DMA
    f32, bf16 = jnp.float32, jnp.bfloat16
    count = len(BATCHES)
    return pl.pallas_call(
        project_kernel,
        out_shape=pltpu.VMEM((2, 4, 4, 7, 8, TILE, LANES), bf16),
        in_specs=[hbm, hbm, hbm],
        out_specs=vmem,
        scratch_shapes=[
            pltpu.VMEM(eig.shape, f32),
            pltpu.VMEM((rows, feats), bf16),
            pltpu.VMEM((rows, feats), bf16),
            pltpu.VMEM((4, feats, LANES), bf16),
            pltpu.VMEM((7, 8, TILE, 4 * LANES), f32),
            pltpu.VMEM((7, 7, TILE, 4 * LANES), f32),
            pltpu.VMEM((4, 7, TILE, LANES), f32),
            pltpu.VMEM((3, 7, TILE, LANES), f32),
            dma((3,)),
            dma((3 + CHUNKS,)), dma((3 + CHUNKS,)),
            dma((2, CHUNKS)), dma((2, CHUNKS)),
            dma((CHUNKS,)), dma((CHUNKS,)),
            dma((count, 7)), dma((count, 7)),
            dma((count, 3)), dma((count, 3)),
            dma((count, 7)), dma((count, 7)),
            dma((count, 15)), dma((count, 15)),
            dma((count,)), dma((count,)),
        ],
        compiler_params=pltpu.CompilerParams(
            collective_id=0, has_side_effects=True, vmem_limit_bytes=40 << 20
        ),
    )(*(pltpu.with_memory_space_constraint(a, pltpu.HBM) for a in (g, b, eig)))


HALF = 224


def score_kernel(first, w, store, index, out):
    columns = out.shape[1]
    half = pl.program_id(0) // 4
    x = lax.rem(pl.program_id(0), 4)
    here = first[0] + lax.broadcasted_iota(jnp.int32, (LANES, columns), 1)

    def tile(shift):
        wide = []
        for q in range(2):
            lines = pl.ds(pl.multiple_of((half if q == 0 else 1 - half) * HALF, 32), HALF)
            for c in range(4):
                p = [t % 4 for t in TURNS].index((c - shift) % 4)
                wide.append(w[q, p, shift, lines])
        return jnp.concatenate(wide, axis=1)

    for shift in range(4):

        @pl.when(x == shift)
        def _():
            product = lax.dot_general(
                tile(shift), store[...], (((1,), (1,)), ((), ())),
                preferred_element_type=jnp.float32,
            )
            out[...] = product

    for start in range(0, HALF, LANES):
        count = min(LANES, HALF - start)
        line = index[pl.program_id(0), :, start : start + LANES]
        wanted = jnp.broadcast_to(line, (LANES, LANES)).T[:count]
        wanted = jnp.concatenate([wanted] * (columns // LANES), axis=1)
        lines = slice(start, start + count)
        out[lines, :] = jnp.where(wanted == here[:count], 0.0, out[lines, :])


def score(first, w, store, index):
    columns, depth = store.shape
    count = index.shape[0] * HALF
    return pl.pallas_call(
        score_kernel,
        out_shape=jax.ShapeDtypeStruct((count, columns), jnp.float32),
        grid=(index.shape[0],),
        in_specs=[
            pl.BlockSpec(memory_space=pltpu.SMEM),
            pl.BlockSpec(memory_space=pltpu.VMEM),
            pl.BlockSpec(memory_space=pltpu.VMEM),
            pl.BlockSpec(memory_space=pltpu.VMEM),
        ],
        out_specs=pl.BlockSpec((HALF, columns), lambda i: (i, 0)),
        compiler_params=pltpu.CompilerParams(vmem_limit_bytes=24 << 20),
    )(first, w, store, index)


def shards(slab_grads, basis, eigenvalues, store_rows, slab_index):
    zl, x, y, zh, core = (lax.axis_index(a) for a in AXES)
    place = (((zl * 4 + x) * 4 + y) * 4 + zh) * 2 + core
    first = (place * store_rows.shape[0]).astype(jnp.int32).reshape(1)
    w = project(slab_grads, basis, eigenvalues.reshape(8, LANES))
    w = w.reshape(2, 4, 4, 7 * BLOCK, LANES)
    index = jnp.pad(slab_index.reshape(8, 1, HALF), ((0, 0), (0, 0), (0, 2 * LANES - HALF)))
    return score(first, w, store_rows, index)


def solution(mesh):
    split = Mesh(mesh.devices.reshape(2, 4, 4, 4, 2), AXES)
    rows, feat = ("zl", "x"), ("y", "zh", "core")
    placed = (P(rows, feat), P(feat, rows), P(), P(rows + feat, None), P())
    return jax.shard_map(
        shards, mesh=split, in_specs=placed, out_specs=P(None, rows + feat), check_vma=False
    )
```

```python
import jax
import jax.numpy as jnp
from jax import lax
from jax.experimental import pallas as pl
from jax.experimental.pallas import tpu as pltpu
from jax.sharding import Mesh
from jax.sharding import PartitionSpec as P

AXES = ("zl", "x", "y", "zh", "core")
SIZES = {"zl": 2, "x": 4, "y": 4, "zh": 4, "core": 2}
MESH = pl.DeviceIdType.MESH
DAMPING = 0.1
CHUNKS = 8
LANES = 128
TILE = 8
BLOCK = 64
TURNS = (0, -1, 1, 2)
NEAR_ROWS = ((0, 32), (32, 96), (96, 160))
LAST_ROWS = (160, 224)
EARLY, ACROSS, FIFTH, SIXTH = (0, 5, 0, 3), (0, 5, 3, 4), (5, 6, 0, 4), (6, 7, 0, 4)
BATCHES = (EARLY, ACROSS, FIFTH, SIXTH)


def turned(axis, by):
    return lax.rem(lax.axis_index(axis) + (by % SIZES[axis]), SIZES[axis])


def project_kernel(
    g, b, eig_in, w,
    eig, g_own, g_pair, b_all, acc, r1, s1, r2, w0, w1, w2, w3,
    local_sem, g_send, g_recv, b_send, b_recv, f_send, f_recv,
    a_send, a_recv, c_send, c_recv, e_send, e_recv, h_send, h_recv, k_send, k_recv,
):
    rows, feats = g.shape
    step = feats // CHUNKS
    zl, x, y, zh, core = (lax.axis_index(a) for a in AXES)
    pair, sibling = {"zl": 1 - zl}, {"core": 1 - core}
    right, left = {"x": turned("x", 1)}, {"x": turned("x", -1)}
    mine = core * 4 + y

    plane = [(dy, dc) for dy in (2, 1, 3) for dc in (0, 1)] + [(0, 1)]
    deep = [2, 1, 3]
    column = [(dl, dh) for dh in (2, 1, 3, 0) for dl in (0, 1) if dl or dh]
    sheet = [(dx, dy) for dx in (2, 1, 3, 0) for dy in (2, 1, 3, 0) if dx or dy]

    def flipped(value, by):
        return 1 - value if by else value

    def plane_peer(o):
        return {"y": turned("y", o[0]), "core": flipped(core, o[1])}

    def column_peer(o):
        return {"zl": flipped(zl, o[0]), "zh": turned("zh", o[1])}

    def sheet_peer(o):
        return {"x": turned("x", o[0]), "y": turned("y", o[1])}

    barrier = pltpu.get_barrier_semaphore()
    everyone = (
        [column_peer(o) for o in column]
        + [sheet_peer(o) for o in sheet]
        + [plane_peer(o) for o in plane if o[1]]
    )
    for peer in everyone:
        pl.semaphore_signal(barrier, inc=1, device_id=peer, device_id_type=MESH)
    locals_ = [
        pltpu.make_async_copy(b, b_all.at[0], local_sem.at[0]),
        pltpu.make_async_copy(g, g_own, local_sem.at[1]),
        pltpu.make_async_copy(eig_in, eig, local_sem.at[2]),
    ]
    for copy in locals_:
        copy.start()
    pl.semaphore_wait(barrier, len(everyone))

    def remote(src, dst, send, recv, peer):
        return pltpu.make_async_remote_copy(
            src_ref=src, dst_ref=dst, send_sem=send, recv_sem=recv,
            device_id=peer, device_id_type=MESH,
        )

    def part_of(k):
        return pl.ds(pl.multiple_of(k * step, step), step)

    def near_copy(i):
        lines = slice(*NEAR_ROWS[i])
        return remote(g.at[lines], g_pair.at[lines], g_send.at[i], g_recv.at[i], pair)

    def last_copy(k):
        place = (slice(*LAST_ROWS), part_of(k))
        return remote(g.at[place], g_pair.at[place], g_send.at[3 + k], g_recv.at[3 + k], pair)

    def b_copy(side, k):
        return remote(
            b.at[part_of(k)], b_all.at[1 + side, part_of(k)],
            b_send.at[side, k], b_recv.at[side, k], left if side else right,
        )

    def forward(side, k):
        return remote(
            b_all.at[1 + side, part_of(k)], b_all.at[3, part_of(k)],
            f_send.at[k], f_recv.at[k], left if side else right,
        )

    near_copy(0).start()
    for i in range(1, 3):
        near_copy(i).start()

    @pl.loop(0, CHUNKS)
    def _(k):
        b_copy(0, k).start()
        b_copy(1, k).start()
        last_copy(k).start()

    def dot(lhs, rhs):
        out = jnp.dot(lhs, rhs, preferred_element_type=jnp.float32)
        return out.reshape(-1, TILE, out.shape[1])

    def joined(places, k):
        return jnp.concatenate([b_all[i, part_of(k)] for i in places], axis=1)

    def add_own(k, rhs, lanes):
        out = dot(g_own[:, part_of(k)], rhs)
        acc[0:3, :, :, lanes] += out[:24].reshape(3, 8, TILE, -1)
        acc[3, 0:4, :, lanes] += out[24:]

    def add_pair(k, rhs, lanes):
        out = dot(g_pair[0:96, part_of(k)], rhs)
        acc[3, 4:8, :, lanes] += out[:4]
        acc[4, :, :, lanes] += out[4:]

    def add_block(block, k):
        first = block * BLOCK - rows
        out = dot(g_pair[first : first + BLOCK, part_of(k)], joined(range(4), k))
        acc[block] += out

    acc[...] = jnp.zeros_like(acc)
    for copy in locals_:
        copy.wait()

    started = []
    parts = (w0, w1, w2, w3)

    def go(copy):
        copy.start()
        started.append(copy)
        return copy

    def lanes_of(batch):
        return slice(batch[2] * LANES, batch[3] * LANES)

    def reduce_plane(n):
        batch = BATCHES[n]
        blocks, lanes = slice(*batch[:2]), lanes_of(batch)
        copies = []
        for i, o in enumerate(plane):
            peer = plane_peer(o)
            theirs = peer["core"] * 4 + peer["y"]
            copies.append(
                go(remote(
                    acc.at[blocks, theirs, :, lanes], r1.at[i, blocks, :, lanes],
                    a_send.at[n, i], a_recv.at[n, i], peer,
                ))
            )
        return copies

    def within(place, batch):
        if batch[2:] == (0, 4):
            return None
        return jnp.logical_and(place >= batch[2], place < batch[3])

    def guarded(condition, body):
        if condition is None:
            body()
        else:
            pl.when(condition)(body)

    def deep_copy(n, i):
        batch = BATCHES[n]
        blocks, there = slice(*batch[:2]), turned("zh", deep[i])
        return remote(
            s1.at[there, blocks], r2.at[i, blocks], c_send.at[n, i], c_recv.at[n, i], {"zh": there}
        )

    def reduce_deep(n, copies):
        batch = BATCHES[n]
        blocks = slice(*batch[:2])
        for copy in copies:
            copy.wait_recv()
        for p in range(batch[2], batch[3]):
            lanes = slice(p * LANES, (p + 1) * LANES)
            total = acc[blocks, mine, :, lanes]
            for i in range(len(plane)):
                total = total + r1[i, blocks, :, lanes]
            s1[p, blocks] = total
        for i in range(len(deep)):
            guarded(within(turned("zh", deep[i]), batch), lambda i=i: deep_copy(n, i).start())

    def own_place(n):
        return parts[n].at[x, mine, zl, zh - BATCHES[n][2]]

    def column_copy(n, i):
        place = own_place(n)
        return remote(place, place, e_send.at[n, i], e_recv.at[n, i], column_peer(column[i]))

    def column_arrival(n, i):
        place = parts[n].at[x, mine, 0, 0]
        return remote(place, place, e_send.at[n, i], e_recv.at[n, i], column_peer(column[i]))

    def spread_column(n):
        batch = BATCHES[n]
        blocks = slice(*batch[:2])

        def body():
            for i in range(len(deep)):
                deep_copy(n, i).wait_recv()
            total = s1[zh, blocks]
            for i in range(len(deep)):
                total = total + r2[i, blocks]
            turn = jnp.where(zh == 0, 0, jnp.where(zh == 1, 3, jnp.where(zh == 2, 1, 2)))
            scale = eig[pl.ds(zl * 4 + lax.rem(x + turn, 4), 1), :] + DAMPING
            parts[n][x, mine, zl, zh - batch[2]] = (total / scale[None]).astype(w.dtype)
            for i in range(len(column)):
                column_copy(n, i).start()

        guarded(within(zh, batch), body)

    def spread_sheet(n):
        batch = BATCHES[n]
        for i, (_, dh) in enumerate(column):
            guarded(
                within(turned("zh", -dh), batch), lambda i=i: column_arrival(n, i).wait_recv()
            )
        place = parts[n].at[x, mine]
        return [
            go(remote(place, place, h_send.at[n, i], h_recv.at[n, i], sheet_peer(o)))
            for i, o in enumerate(sheet)
        ]

    def share(n, copies):
        for copy in copies:
            copy.wait_recv()
        place = parts[n].at[:, pl.ds(core * 4, 4)]
        return go(remote(place, place, k_send.at[n], k_recv.at[n], sibling))

    def place_tiles(n, copy):
        first, last, low, high = BATCHES[n]
        copy.wait_recv()

        @pl.loop(0, 32)
        def _(i):
            row, lot = i // 8, lax.rem(i, 8)
            for q in range(2):
                for p in range(low, high):
                    w[q, p, row, first:last, lot] = parts[n][row, lot, q, p - low]

    @pl.loop(0, CHUNKS // 2)
    def _(pairs):
        for odd in (0, 1):
            k = pairs * 2 + odd
            b_copy(0, k).wait_recv()
            b_copy(1, k).wait_recv()
            forward(odd, k).start()
            add_own(k, joined(range(3), k), slice(0, 3 * LANES))

    near_copy(0).wait_recv()
    near_copy(1).wait_recv()

    @pl.loop(0, CHUNKS)
    def _(k):
        add_pair(k, joined(range(3), k), slice(0, 3 * LANES))

    early = reduce_plane(0)
    reduce_deep(0, early)
    spread_column(0)

    @pl.loop(0, CHUNKS)
    def _(k):
        forward(0, k).wait_recv()
        add_own(k, b_all[3, part_of(k)], slice(3 * LANES, 4 * LANES))
        add_pair(k, b_all[3, part_of(k)], slice(3 * LANES, 4 * LANES))

    across = reduce_plane(1)
    near_copy(2).wait_recv()

    @pl.loop(0, CHUNKS)
    def _(k):
        add_block(5, k)

    fifth = reduce_plane(2)
    early = spread_sheet(0)
    reduce_deep(1, across)
    reduce_deep(2, fifth)

    @pl.loop(0, CHUNKS)
    def _(k):
        last_copy(k).wait_recv()
        add_block(6, k)

    sixth = reduce_plane(3)
    spread_column(1)
    spread_column(2)
    reduce_deep(3, sixth)
    across = spread_sheet(1)
    fifth = spread_sheet(2)
    spread_column(3)
    early = share(0, early)
    sixth = spread_sheet(3)
    place_tiles(0, early)
    across = share(1, across)
    fifth = share(2, fifth)
    place_tiles(1, across)
    place_tiles(2, fifth)
    place_tiles(3, share(3, sixth))

    for i in range(3):
        near_copy(i).wait_send()

    @pl.loop(0, CHUNKS)
    def _(k):
        last_copy(k).wait_send()
        b_copy(0, k).wait_send()
        b_copy(1, k).wait_send()
        forward(0, k).wait_send()

    for n, batch in enumerate(BATCHES):
        for i in range(len(deep)):
            guarded(within(turned("zh", deep[i]), batch), lambda: deep_copy(n, i).wait_send())

        def body():
            for i in range(len(column)):
                column_copy(n, i).wait_send()

        guarded(within(zh, batch), body)
    for copy in started:
        copy.wait_send()


def project(g, b, eig):
    rows, feats = g.shape
    hbm = pl.BlockSpec(memory_space=pltpu.HBM)
    vmem = pl.BlockSpec(memory_space=pltpu.VMEM)
    dma = pltpu.SemaphoreType.DMA
    f32, bf16 = jnp.float32, jnp.bfloat16
    count = len(BATCHES)
    return pl.pallas_call(
        project_kernel,
        out_shape=pltpu.VMEM((2, 4, 4, 7, 8, TILE, LANES), bf16),
        in_specs=[hbm, hbm, hbm],
        out_specs=vmem,
        scratch_shapes=[
            pltpu.VMEM(eig.shape, f32),
            pltpu.VMEM((rows, feats), bf16),
            pltpu.VMEM((rows, feats), bf16),
            pltpu.VMEM((4, feats, LANES), bf16),
            pltpu.VMEM((7, 8, TILE, 4 * LANES), f32),
            pltpu.VMEM((7, 7, TILE, 4 * LANES), f32),
            pltpu.VMEM((4, 7, TILE, LANES), f32),
            pltpu.VMEM((3, 7, TILE, LANES), f32),
            *(
                pltpu.VMEM((4, 8, 2, high - low, last - first, TILE, LANES), bf16)
                for first, last, low, high in BATCHES
            ),
            dma((3,)),
            dma((3 + CHUNKS,)), dma((3 + CHUNKS,)),
            dma((2, CHUNKS)), dma((2, CHUNKS)),
            dma((CHUNKS,)), dma((CHUNKS,)),
            dma((count, 7)), dma((count, 7)),
            dma((count, 3)), dma((count, 3)),
            dma((count, 7)), dma((count, 7)),
            dma((count, 15)), dma((count, 15)),
            dma((count,)), dma((count,)),
        ],
        compiler_params=pltpu.CompilerParams(
            collective_id=0, has_side_effects=True, vmem_limit_bytes=40 << 20
        ),
    )(*(pltpu.with_memory_space_constraint(a, pltpu.HBM) for a in (g, b, eig)))


HALF = 224
STEPS = 4


def score_kernel(first, w, store, index, out):
    columns = out.shape[1]
    here = first[0] + lax.broadcasted_iota(jnp.int32, (HALF, LANES), 1)

    def wide(half, x):
        pieces = []
        for q in range(2):
            start = (half if q == 0 else 1 - half) * HALF
            for c in range(4):
                p = [t % 4 for t in TURNS].index((c - x) % 4)
                pieces.append(w[q, p, x, start : start + HALF])
        return jnp.concatenate(pieces, axis=1)

    def wanted(block):
        lines, stop = [], (block + 1) * HALF
        row = block * HALF
        while row < stop:
            tile = row // LANES * LANES
            end = min(stop, tile + LANES)
            line = index[tile : tile + LANES].reshape(1, LANES)
            lines.append(jnp.broadcast_to(line, (LANES, LANES)).T[row - tile : end - tile])
            row = end
        return jnp.concatenate(lines, axis=0)

    for step in range(STEPS):

        @pl.when(pl.program_id(0) == step)
        def _():
            for i in range(8 // STEPS):
                block = step * (8 // STEPS) + i
                product = lax.dot_general(
                    wide(block // 4, block % 4), store[...], (((1,), (1,)), ((), ())),
                    preferred_element_type=jnp.float32,
                )
                hit = wanted(block) - here
                lines = slice(i * HALF, (i + 1) * HALF)
                for n in range(0, columns, LANES):
                    lanes = slice(n, n + LANES)
                    out[lines, lanes] = jnp.where(hit == n, 0.0, product[:, lanes])


def score(first, w, store, index):
    columns, depth = store.shape
    count = index.shape[0]
    vmem = pl.BlockSpec(memory_space=pltpu.VMEM)
    return pl.pallas_call(
        score_kernel,
        out_shape=jax.ShapeDtypeStruct((count, columns), jnp.float32),
        grid=(STEPS,),
        in_specs=[pl.BlockSpec(memory_space=pltpu.SMEM), vmem, vmem, vmem],
        out_specs=pl.BlockSpec((count // STEPS, columns), lambda i: (i, 0)),
        compiler_params=pltpu.CompilerParams(vmem_limit_bytes=24 << 20),
    )(first, w, store, index)


def shards(slab_grads, basis, eigenvalues, store_rows, slab_index):
    zl, x, y, zh, core = (lax.axis_index(a) for a in AXES)
    place = (((zl * 4 + x) * 4 + y) * 4 + zh) * 2 + core
    first = (place * store_rows.shape[0]).astype(jnp.int32).reshape(1)
    w = project(slab_grads, basis, eigenvalues.reshape(8, LANES))
    w = w.reshape(2, 4, 4, 7 * BLOCK, LANES)
    return score(first, w, store_rows, slab_index)


def solution(mesh):
    split = Mesh(mesh.devices.reshape(2, 4, 4, 4, 2), AXES)
    rows, feat = ("zl", "x"), ("y", "zh", "core")
    placed = (P(rows, feat), P(feat, rows), P(), P(rows + feat, None), P())
    return jax.shard_map(
        shards, mesh=split, in_specs=placed, out_specs=P(None, rows + feat), check_vma=False
    )
```

```python
import jax
import jax.numpy as jnp
from jax import lax
from jax.experimental import pallas as pl
from jax.experimental.pallas import tpu as pltpu
from jax.sharding import Mesh
from jax.sharding import PartitionSpec as P

AXES = ("zl", "x", "y", "zh", "core")
SIZES = {"zl": 2, "x": 4, "y": 4, "zh": 4, "core": 2}
MESH = pl.DeviceIdType.MESH
DAMPING = 0.1
CHUNKS = 8
LANES = 128
TILE = 8
BLOCK = 64
ROUNDS = 3
TURNS = (0, -1, 1, 2)
NEAR_ROWS = ((0, 32), (32, 96), (96, 160))
LAST_ROWS = (160, 224)
EARLY, ACROSS, FIFTH, SIXTH = (0, 5, 0, 3), (0, 5, 3, 4), (5, 6, 0, 4), (6, 7, 0, 4)
BATCHES = (EARLY, ACROSS, FIFTH, SIXTH)


def turned(axis, by):
    return lax.rem(lax.axis_index(axis) + (by % SIZES[axis]), SIZES[axis])


def project_kernel(
    g, b, eig_in, w,
    eig, g_own, g_pair, b_all, acc, r1, s1, r2, w0, w1, w2, w3,
    ready, local_sem, g_send, g_recv, b_send, b_recv, f_send, f_recv,
    a_send, a_recv, c_send, c_recv, e_send, e_recv, h_send, h_recv, k_send, k_recv,
):
    rows, feats = g.shape
    step = feats // CHUNKS
    zl, x, y, zh, core = (lax.axis_index(a) for a in AXES)
    pair, sibling = {"zl": 1 - zl}, {"core": 1 - core}
    right, left = {"x": turned("x", 1)}, {"x": turned("x", -1)}
    mine = core * 4 + y

    plane = [(dy, dc) for dy in (2, 1, 3) for dc in (0, 1)] + [(0, 1)]
    deep = [2, 1, 3]
    column = [(dl, dh) for dh in (2, 1, 3, 0) for dl in (0, 1) if dl or dh]
    sheet = [(dx, dy) for dx in (2, 1, 3, 0) for dy in (2, 1, 3, 0) if dx or dy]

    def flipped(value, by):
        return 1 - value if by else value

    def plane_peer(o):
        return {"y": turned("y", o[0]), "core": flipped(core, o[1])}

    def column_peer(o):
        return {"zl": flipped(zl, o[0]), "zh": turned("zh", o[1])}

    def sheet_peer(o):
        return {"x": turned("x", o[0]), "y": turned("y", o[1])}

    barrier = pltpu.get_barrier_semaphore()
    beside = {"zl": 1 - zl, "zh": lax.rem(zh + 2 * zl + 3, 4)}
    nearest = [pair, right, left, {"y": turned("y", 1)}, {"y": turned("y", -1)}, beside, sibling]

    def meet(semaphore):
        for peer in nearest:
            pl.semaphore_signal(semaphore, inc=1, device_id=peer, device_id_type=MESH)

    meet(barrier)
    locals_ = [
        pltpu.make_async_copy(b, b_all.at[0], local_sem.at[0]),
        pltpu.make_async_copy(g, g_own, local_sem.at[1]),
        pltpu.make_async_copy(eig_in, eig, local_sem.at[2]),
    ]
    for copy in locals_:
        copy.start()
    pl.semaphore_wait(barrier, len(nearest))

    def remote(src, dst, send, recv, peer):
        return pltpu.make_async_remote_copy(
            src_ref=src, dst_ref=dst, send_sem=send, recv_sem=recv,
            device_id=peer, device_id_type=MESH,
        )

    def part_of(k):
        return pl.ds(pl.multiple_of(k * step, step), step)

    def near_copy(i):
        lines = slice(*NEAR_ROWS[i])
        return remote(g.at[lines], g_pair.at[lines], g_send.at[i], g_recv.at[i], pair)

    def last_copy(k):
        place = (slice(*LAST_ROWS), part_of(k))
        return remote(g.at[place], g_pair.at[place], g_send.at[3 + k], g_recv.at[3 + k], pair)

    def b_copy(side, k):
        return remote(
            b.at[part_of(k)], b_all.at[1 + side, part_of(k)],
            b_send.at[side, k], b_recv.at[side, k], left if side else right,
        )

    def forward(side, k):
        return remote(
            b_all.at[1 + side, part_of(k)], b_all.at[3, part_of(k)],
            f_send.at[k], f_recv.at[k], left if side else right,
        )

    near_copy(0).start()
    for i in range(1, 3):
        near_copy(i).start()

    @pl.loop(0, CHUNKS)
    def _(k):
        b_copy(0, k).start()
        b_copy(1, k).start()
        last_copy(k).start()

    for r in range(ROUNDS):
        meet(ready.at[r])
        pl.semaphore_wait(ready.at[r], len(nearest))

    def dot(lhs, rhs):
        out = jnp.dot(lhs, rhs, preferred_element_type=jnp.float32)
        return out.reshape(-1, TILE, out.shape[1])

    def joined(places, k):
        return jnp.concatenate([b_all[i, part_of(k)] for i in places], axis=1)

    def add_own(k, rhs, lanes):
        out = dot(g_own[:, part_of(k)], rhs)
        acc[0:3, :, :, lanes] += out[:24].reshape(3, 8, TILE, -1)
        acc[3, 0:4, :, lanes] += out[24:]

    def add_pair(k, rhs, lanes):
        out = dot(g_pair[0:96, part_of(k)], rhs)
        acc[3, 4:8, :, lanes] += out[:4]
        acc[4, :, :, lanes] += out[4:]

    def add_block(block, k):
        first = block * BLOCK - rows
        out = dot(g_pair[first : first + BLOCK, part_of(k)], joined(range(4), k))
        acc[block] += out

    acc[...] = jnp.zeros_like(acc)
    for copy in locals_:
        copy.wait()

    started = []
    parts = (w0, w1, w2, w3)

    def go(copy):
        copy.start()
        started.append(copy)
        return copy

    def lanes_of(batch):
        return slice(batch[2] * LANES, batch[3] * LANES)

    def reduce_plane(n):
        batch = BATCHES[n]
        blocks, lanes = slice(*batch[:2]), lanes_of(batch)
        copies = []
        for i, o in enumerate(plane):
            peer = plane_peer(o)
            theirs = peer["core"] * 4 + peer["y"]
            copies.append(
                go(remote(
                    acc.at[blocks, theirs, :, lanes], r1.at[i, blocks, :, lanes],
                    a_send.at[n, i], a_recv.at[n, i], peer,
                ))
            )
        return copies

    def within(place, batch):
        if batch[2:] == (0, 4):
            return None
        return jnp.logical_and(place >= batch[2], place < batch[3])

    def guarded(condition, body):
        if condition is None:
            body()
        else:
            pl.when(condition)(body)

    def deep_copy(n, i):
        batch = BATCHES[n]
        blocks, there = slice(*batch[:2]), turned("zh", deep[i])
        return remote(
            s1.at[there, blocks], r2.at[i, blocks], c_send.at[n, i], c_recv.at[n, i], {"zh": there}
        )

    def reduce_deep(n, copies):
        batch = BATCHES[n]
        blocks = slice(*batch[:2])
        for copy in copies:
            copy.wait_recv()
        for p in range(batch[2], batch[3]):
            lanes = slice(p * LANES, (p + 1) * LANES)
            total = acc[blocks, mine, :, lanes]
            for i in range(len(plane)):
                total = total + r1[i, blocks, :, lanes]
            s1[p, blocks] = total
        for i in range(len(deep)):
            guarded(within(turned("zh", deep[i]), batch), lambda i=i: deep_copy(n, i).start())

    def own_place(n):
        return parts[n].at[x, mine, zl, zh - BATCHES[n][2]]

    def column_copy(n, i):
        place = own_place(n)
        return remote(place, place, e_send.at[n, i], e_recv.at[n, i], column_peer(column[i]))

    def column_arrival(n, i):
        place = parts[n].at[x, mine, 0, 0]
        return remote(place, place, e_send.at[n, i], e_recv.at[n, i], column_peer(column[i]))

    def spread_column(n):
        batch = BATCHES[n]
        blocks = slice(*batch[:2])

        def body():
            for i in range(len(deep)):
                deep_copy(n, i).wait_recv()
            total = s1[zh, blocks]
            for i in range(len(deep)):
                total = total + r2[i, blocks]
            turn = jnp.where(zh == 0, 0, jnp.where(zh == 1, 3, jnp.where(zh == 2, 1, 2)))
            scale = eig[pl.ds(zl * 4 + lax.rem(x + turn, 4), 1), :] + DAMPING
            parts[n][x, mine, zl, zh - batch[2]] = (total / scale[None]).astype(w.dtype)
            for i in range(len(column)):
                column_copy(n, i).start()

        guarded(within(zh, batch), body)

    def spread(n, place, peers, first):
        return [
            go(remote(
                place, place, h_send.at[n, first + i], h_recv.at[n, first + i], peer
            ))
            for i, peer in enumerate(peers)
        ]

    def settle_column(n):
        for i, (_, dh) in enumerate(column):
            guarded(
                within(turned("zh", -dh), BATCHES[n]),
                lambda i=i: column_arrival(n, i).wait_recv(),
            )

    def spread_sheet(n):
        settle_column(n)
        return spread(n, parts[n].at[x, mine], [sheet_peer(o) for o in sheet], 0)

    x_peers = [{"x": turned("x", d)} for d in deep]
    y_peers = [{"y": turned("y", d)} for d in deep]

    def spread_first(n):
        settle_column(n)
        part = parts[n]
        return spread(n, part.at[x, mine, 0], x_peers, 0) + spread(n, part.at[x, mine, 1], y_peers, 3)

    def spread_second(n, copies):
        for copy in copies:
            copy.wait_recv()
        part = parts[n]
        return spread(n, part.at[:, mine, 0], y_peers, 6) + spread(
            n, part.at[x, pl.ds(core * 4, 4), 1], x_peers, 9
        )

    def share(n, copies):
        for copy in copies:
            copy.wait_recv()
        place = parts[n].at[:, pl.ds(core * 4, 4)]
        return go(remote(place, place, k_send.at[n], k_recv.at[n], sibling))

    def place_tiles(n, copy):
        first, last, low, high = BATCHES[n]
        copy.wait_recv()

        @pl.loop(0, 32)
        def _(i):
            row, lot = i // 8, lax.rem(i, 8)
            for q in range(2):
                for p in range(low, high):
                    w[q, p, row, first:last, lot] = parts[n][row, lot, q, p - low]

    @pl.loop(0, CHUNKS)
    def _(k):
        b_copy(0, k).wait_recv()
        b_copy(1, k).wait_recv()
        add_own(k, joined(range(3), k), slice(0, 3 * LANES))

    @pl.loop(0, CHUNKS // 2)
    def _(pairs):
        for odd in (0, 1):
            forward(odd, pairs * 2 + odd).start()

    near_copy(0).wait_recv()
    near_copy(1).wait_recv()

    @pl.loop(0, CHUNKS)
    def _(k):
        add_pair(k, joined(range(3), k), slice(0, 3 * LANES))

    early = reduce_plane(0)

    @pl.loop(0, CHUNKS)
    def _(k):
        forward(0, k).wait_recv()
        add_own(k, b_all[3, part_of(k)], slice(3 * LANES, 4 * LANES))
        add_pair(k, b_all[3, part_of(k)], slice(3 * LANES, 4 * LANES))

    across = reduce_plane(1)
    near_copy(2).wait_recv()

    @pl.loop(0, CHUNKS)
    def _(k):
        add_block(5, k)

    fifth = reduce_plane(2)
    reduce_deep(0, early)
    reduce_deep(1, across)
    reduce_deep(2, fifth)

    @pl.loop(0, CHUNKS)
    def _(k):
        last_copy(k).wait_recv()
        add_block(6, k)

    sixth = reduce_plane(3)
    spread_column(0)
    spread_column(1)
    spread_column(2)
    reduce_deep(3, sixth)
    early = spread_first(0)
    across = spread_first(1)
    fifth = spread_first(2)
    spread_column(3)
    early = spread_second(0, early)
    across = spread_second(1, across)
    fifth = spread_second(2, fifth)
    sixth = spread_sheet(3)
    early = share(0, early)
    place_tiles(0, early)
    across = share(1, across)
    fifth = share(2, fifth)
    sixth = share(3, sixth)
    place_tiles(1, across)
    place_tiles(2, fifth)
    place_tiles(3, sixth)

    for i in range(3):
        near_copy(i).wait_send()

    @pl.loop(0, CHUNKS)
    def _(k):
        last_copy(k).wait_send()
        b_copy(0, k).wait_send()
        b_copy(1, k).wait_send()
        forward(0, k).wait_send()

    for n, batch in enumerate(BATCHES):
        for i in range(len(deep)):
            guarded(within(turned("zh", deep[i]), batch), lambda: deep_copy(n, i).wait_send())

        def body():
            for i in range(len(column)):
                column_copy(n, i).wait_send()

        guarded(within(zh, batch), body)
    for copy in started:
        copy.wait_send()


def project(g, b, eig):
    rows, feats = g.shape
    hbm = pl.BlockSpec(memory_space=pltpu.HBM)
    vmem = pl.BlockSpec(memory_space=pltpu.VMEM)
    dma = pltpu.SemaphoreType.DMA
    f32, bf16 = jnp.float32, jnp.bfloat16
    count = len(BATCHES)
    return pl.pallas_call(
        project_kernel,
        out_shape=pltpu.VMEM((2, 4, 4, 7, 8, TILE, LANES), bf16),
        in_specs=[hbm, hbm, hbm],
        out_specs=vmem,
        scratch_shapes=[
            pltpu.VMEM(eig.shape, f32),
            pltpu.VMEM((rows, feats), bf16),
            pltpu.VMEM((rows, feats), bf16),
            pltpu.VMEM((4, feats, LANES), bf16),
            pltpu.VMEM((7, 8, TILE, 4 * LANES), f32),
            pltpu.VMEM((7, 7, TILE, 4 * LANES), f32),
            pltpu.VMEM((4, 7, TILE, LANES), f32),
            pltpu.VMEM((3, 7, TILE, LANES), f32),
            *(
                pltpu.VMEM((4, 8, 2, high - low, last - first, TILE, LANES), bf16)
                for first, last, low, high in BATCHES
            ),
            pltpu.SemaphoreType.REGULAR((ROUNDS,)),
            dma((3,)),
            dma((3 + CHUNKS,)), dma((3 + CHUNKS,)),
            dma((2, CHUNKS)), dma((2, CHUNKS)),
            dma((CHUNKS,)), dma((CHUNKS,)),
            dma((count, 7)), dma((count, 7)),
            dma((count, 3)), dma((count, 3)),
            dma((count, 7)), dma((count, 7)),
            dma((count, 15)), dma((count, 15)),
            dma((count,)), dma((count,)),
        ],
        compiler_params=pltpu.CompilerParams(
            collective_id=0, has_side_effects=True, vmem_limit_bytes=40 << 20
        ),
    )(*(pltpu.with_memory_space_constraint(a, pltpu.HBM) for a in (g, b, eig)))


HALF = 224
STEPS = 4


def score_kernel(first, w, store, index, out):
    columns = out.shape[1]
    here = first[0] + lax.broadcasted_iota(jnp.int32, (HALF, LANES), 1)

    def wide(half, x):
        pieces = []
        for q in range(2):
            start = (half if q == 0 else 1 - half) * HALF
            for c in range(4):
                p = [t % 4 for t in TURNS].index((c - x) % 4)
                pieces.append(w[q, p, x, start : start + HALF])
        return jnp.concatenate(pieces, axis=1)

    def wanted(block):
        lines, stop = [], (block + 1) * HALF
        row = block * HALF
        while row < stop:
            tile = row // LANES * LANES
            end = min(stop, tile + LANES)
            line = index[tile : tile + LANES].reshape(1, LANES)
            lines.append(jnp.broadcast_to(line, (LANES, LANES)).T[row - tile : end - tile])
            row = end
        return jnp.concatenate(lines, axis=0)

    for step in range(STEPS):

        @pl.when(pl.program_id(0) == step)
        def _():
            for i in range(8 // STEPS):
                block = step * (8 // STEPS) + i
                product = lax.dot_general(
                    wide(block // 4, block % 4), store[...], (((1,), (1,)), ((), ())),
                    preferred_element_type=jnp.float32,
                )
                hit = wanted(block) - here
                lines = slice(i * HALF, (i + 1) * HALF)
                for n in range(0, columns, LANES):
                    lanes = slice(n, n + LANES)
                    out[lines, lanes] = jnp.where(hit == n, 0.0, product[:, lanes])


def score(first, w, store, index):
    columns, depth = store.shape
    count = index.shape[0]
    vmem = pl.BlockSpec(memory_space=pltpu.VMEM)
    return pl.pallas_call(
        score_kernel,
        out_shape=jax.ShapeDtypeStruct((count, columns), jnp.float32),
        grid=(STEPS,),
        in_specs=[pl.BlockSpec(memory_space=pltpu.SMEM), vmem, vmem, vmem],
        out_specs=pl.BlockSpec((count // STEPS, columns), lambda i: (i, 0)),
        compiler_params=pltpu.CompilerParams(vmem_limit_bytes=24 << 20),
    )(first, w, store, index)


def shards(slab_grads, basis, eigenvalues, store_rows, slab_index):
    zl, x, y, zh, core = (lax.axis_index(a) for a in AXES)
    place = (((zl * 4 + x) * 4 + y) * 4 + zh) * 2 + core
    first = (place * store_rows.shape[0]).astype(jnp.int32).reshape(1)
    w = project(slab_grads, basis, eigenvalues.reshape(8, LANES))
    w = w.reshape(2, 4, 4, 7 * BLOCK, LANES)
    return score(first, w, store_rows, slab_index)


def solution(mesh):
    split = Mesh(mesh.devices.reshape(2, 4, 4, 4, 2), AXES)
    rows, feat = ("zl", "x"), ("y", "zh", "core")
    placed = (P(rows, feat), P(feat, rows), P(), P(rows + feat, None), P())
    return jax.shard_map(
        shards, mesh=split, in_specs=placed, out_specs=P(None, rows + feat), check_vma=False
    )
```

```python
import jax
import jax.numpy as jnp
from jax import lax
from jax.experimental import pallas as pl
from jax.experimental.pallas import tpu as pltpu
from jax.sharding import Mesh
from jax.sharding import PartitionSpec as P

AXES = ("zl", "x", "y", "zh", "core")
SIZES = {"zl": 2, "x": 4, "y": 4, "zh": 4, "core": 2}
MESH = pl.DeviceIdType.MESH
DAMPING = 0.1
CHUNKS = 8
LANES = 128
TILE = 8
BLOCK = 64
ROUNDS = 3
TURNS = (0, -1, 1, 2)
NEAR_ROWS = ((0, 32), (32, 96), (96, 160))
LAST_ROWS = (160, 224)
EARLY, ACROSS, FIFTH, SIXTH = (0, 5, 0, 3), (0, 5, 3, 4), (5, 6, 0, 4), (6, 7, 0, 4)
BATCHES = (EARLY, ACROSS, FIFTH, SIXTH)


def turned(axis, by):
    return lax.rem(lax.axis_index(axis) + (by % SIZES[axis]), SIZES[axis])


def project_kernel(
    g, b, eig_in, w,
    eig, g_own, g_pair, b_all, acc, r1, s1, r2, w0, w1, w2, w3,
    ready, local_sem, g_send, g_recv, b_send, b_recv, f_send, f_recv,
    a_send, a_recv, c_send, c_recv, e_send, e_recv, h_send, h_recv, k_send, k_recv,
):
    rows, feats = g.shape
    step = feats // CHUNKS
    zl, x, y, zh, core = (lax.axis_index(a) for a in AXES)
    pair, sibling = {"zl": 1 - zl}, {"core": 1 - core}
    right, left = {"x": turned("x", 1)}, {"x": turned("x", -1)}
    mine = core * 4 + y

    plane = [(dy, dc) for dy in (2, 1, 3) for dc in (0, 1)] + [(0, 1)]
    deep = [2, 1, 3]
    column = [(dl, dh) for dh in (2, 1, 3, 0) for dl in (0, 1) if dl or dh]
    sheet = [(dx, dy) for dx in (2, 1, 3, 0) for dy in (2, 1, 3, 0) if dx or dy]

    def flipped(value, by):
        return 1 - value if by else value

    def plane_peer(o):
        return {"y": turned("y", o[0]), "core": flipped(core, o[1])}

    def column_peer(o):
        return {"zl": flipped(zl, o[0]), "zh": turned("zh", o[1])}

    def sheet_peer(o):
        return {"x": turned("x", o[0]), "y": turned("y", o[1])}

    barrier = pltpu.get_barrier_semaphore()
    beside = {"zl": 1 - zl, "zh": lax.rem(zh + 2 * zl + 3, 4)}
    nearest = [pair, right, left, {"y": turned("y", 1)}, {"y": turned("y", -1)}, beside, sibling]

    def meet(semaphore):
        for peer in nearest:
            pl.semaphore_signal(semaphore, inc=1, device_id=peer, device_id_type=MESH)

    meet(barrier)
    locals_ = [
        pltpu.make_async_copy(b, b_all.at[0], local_sem.at[0]),
        pltpu.make_async_copy(g, g_own, local_sem.at[1]),
        pltpu.make_async_copy(eig_in, eig, local_sem.at[2]),
    ]
    for copy in locals_:
        copy.start()
    pl.semaphore_wait(barrier, len(nearest))

    def remote(src, dst, send, recv, peer):
        return pltpu.make_async_remote_copy(
            src_ref=src, dst_ref=dst, send_sem=send, recv_sem=recv,
            device_id=peer, device_id_type=MESH,
        )

    def part_of(k):
        return pl.ds(pl.multiple_of(k * step, step), step)

    def near_copy(i):
        lines = slice(*NEAR_ROWS[i])
        return remote(g.at[lines], g_pair.at[lines], g_send.at[i], g_recv.at[i], pair)

    def last_copy(k):
        place = (slice(*LAST_ROWS), part_of(k))
        return remote(g.at[place], g_pair.at[place], g_send.at[3 + k], g_recv.at[3 + k], pair)

    def b_copy(side, k):
        return remote(
            b.at[part_of(k)], b_all.at[1 + side, part_of(k)],
            b_send.at[side, k], b_recv.at[side, k], left if side else right,
        )

    def forward(side, k):
        return remote(
            b_all.at[1 + side, part_of(k)], b_all.at[3, part_of(k)],
            f_send.at[k], f_recv.at[k], left if side else right,
        )

    near_copy(0).start()
    for i in range(1, 3):
        near_copy(i).start()

    @pl.loop(0, CHUNKS)
    def _(k):
        b_copy(0, k).start()
        b_copy(1, k).start()
        last_copy(k).start()

    for r in range(ROUNDS):
        meet(ready.at[r])
        pl.semaphore_wait(ready.at[r], len(nearest))

    def dot(lhs, rhs):
        out = jnp.dot(lhs, rhs, preferred_element_type=jnp.float32)
        return out.reshape(-1, TILE, out.shape[1])

    def joined(places, k):
        return jnp.concatenate([b_all[i, part_of(k)] for i in places], axis=1)

    def add_own(k, rhs, lanes):
        out = dot(g_own[:, part_of(k)], rhs)
        acc[0:3, :, :, lanes] += out[:24].reshape(3, 8, TILE, -1)
        acc[3, 0:4, :, lanes] += out[24:]

    def add_pair(k, rhs, lanes):
        out = dot(g_pair[0:96, part_of(k)], rhs)
        acc[3, 4:8, :, lanes] += out[:4]
        acc[4, :, :, lanes] += out[4:]

    def add_block(block, k):
        first = block * BLOCK - rows
        out = dot(g_pair[first : first + BLOCK, part_of(k)], joined(range(4), k))
        acc[block] += out

    acc[...] = jnp.zeros_like(acc)
    for copy in locals_:
        copy.wait()

    started = []
    parts = (w0, w1, w2, w3)

    def go(copy):
        copy.start()
        started.append(copy)
        return copy

    def lanes_of(batch):
        return slice(batch[2] * LANES, batch[3] * LANES)

    def reduce_plane(n):
        batch = BATCHES[n]
        blocks, lanes = slice(*batch[:2]), lanes_of(batch)
        copies = []
        for i, o in enumerate(plane):
            peer = plane_peer(o)
            theirs = peer["core"] * 4 + peer["y"]
            copies.append(
                go(remote(
                    acc.at[blocks, theirs, :, lanes], r1.at[i, blocks, :, lanes],
                    a_send.at[n, i], a_recv.at[n, i], peer,
                ))
            )
        return copies

    def within(place, batch):
        if batch[2:] == (0, 4):
            return None
        return jnp.logical_and(place >= batch[2], place < batch[3])

    def guarded(condition, body):
        if condition is None:
            body()
        else:
            pl.when(condition)(body)

    def deep_copy(n, i):
        batch = BATCHES[n]
        blocks, there = slice(*batch[:2]), turned("zh", deep[i])
        return remote(
            s1.at[there, blocks], r2.at[i, blocks], c_send.at[n, i], c_recv.at[n, i], {"zh": there}
        )

    def reduce_deep(n, copies):
        batch = BATCHES[n]
        blocks = slice(*batch[:2])
        for copy in copies:
            copy.wait_recv()
        for p in range(batch[2], batch[3]):
            lanes = slice(p * LANES, (p + 1) * LANES)
            total = acc[blocks, mine, :, lanes]
            for i in range(len(plane)):
                total = total + r1[i, blocks, :, lanes]
            s1[p, blocks] = total
        for i in range(len(deep)):
            guarded(within(turned("zh", deep[i]), batch), lambda i=i: deep_copy(n, i).start())

    def own_place(n):
        return parts[n].at[x, mine, zl, zh - BATCHES[n][2]]

    def column_copy(n, i):
        place = own_place(n)
        return remote(place, place, e_send.at[n, i], e_recv.at[n, i], column_peer(column[i]))

    def column_arrival(n, i):
        place = parts[n].at[x, mine, 0, 0]
        return remote(place, place, e_send.at[n, i], e_recv.at[n, i], column_peer(column[i]))

    def spread_column(n):
        batch = BATCHES[n]
        blocks = slice(*batch[:2])

        def body():
            for i in range(len(deep)):
                deep_copy(n, i).wait_recv()
            total = s1[zh, blocks]
            for i in range(len(deep)):
                total = total + r2[i, blocks]
            turn = jnp.where(zh == 0, 0, jnp.where(zh == 1, 3, jnp.where(zh == 2, 1, 2)))
            scale = eig[pl.ds(zl * 4 + lax.rem(x + turn, 4), 1), :] + DAMPING
            parts[n][x, mine, zl, zh - batch[2]] = (total / scale[None]).astype(w.dtype)
            for i in range(len(column)):
                column_copy(n, i).start()

        guarded(within(zh, batch), body)

    def spread(n, place, peers, first):
        return [
            go(remote(
                place, place, h_send.at[n, first + i], h_recv.at[n, first + i], peer
            ))
            for i, peer in enumerate(peers)
        ]

    def settle_column(n):
        for i, (_, dh) in enumerate(column):
            guarded(
                within(turned("zh", -dh), BATCHES[n]),
                lambda i=i: column_arrival(n, i).wait_recv(),
            )

    def spread_sheet(n):
        settle_column(n)
        return spread(n, parts[n].at[x, mine], [sheet_peer(o) for o in sheet], 0)

    x_peers = [{"x": turned("x", d)} for d in deep]
    y_peers = [{"y": turned("y", d)} for d in deep]

    def spread_first(n):
        settle_column(n)
        part = parts[n]
        return spread(n, part.at[x, mine, 0], x_peers, 0) + spread(n, part.at[x, mine, 1], y_peers, 3)

    def spread_second(n, copies):
        for copy in copies:
            copy.wait_recv()
        part = parts[n]
        return spread(n, part.at[:, mine, 0], y_peers, 6) + spread(
            n, part.at[x, pl.ds(core * 4, 4), 1], x_peers, 9
        )

    def share(n, copies):
        for copy in copies:
            copy.wait_recv()
        place = parts[n].at[:, pl.ds(core * 4, 4)]
        return go(remote(place, place, k_send.at[n], k_recv.at[n], sibling))

    def place_tiles(n, copy):
        first, last, low, high = BATCHES[n]
        copy.wait_recv()

        @pl.loop(0, 32)
        def _(i):
            row, lot = i // 8, lax.rem(i, 8)
            for q in range(2):
                for p in range(low, high):
                    w[q, p, row, first:last, lot] = parts[n][row, lot, q, p - low]

    @pl.loop(0, CHUNKS)
    def _(k):
        b_copy(0, k).wait_recv()
        b_copy(1, k).wait_recv()
        add_own(k, joined(range(3), k), slice(0, 3 * LANES))

    @pl.loop(0, CHUNKS // 2)
    def _(pairs):
        for odd in (0, 1):
            forward(odd, pairs * 2 + odd).start()

    near_copy(0).wait_recv()
    near_copy(1).wait_recv()

    @pl.loop(0, CHUNKS)
    def _(k):
        add_pair(k, joined(range(3), k), slice(0, 3 * LANES))

    early = reduce_plane(0)

    @pl.loop(0, CHUNKS)
    def _(k):
        forward(0, k).wait_recv()
        add_own(k, b_all[3, part_of(k)], slice(3 * LANES, 4 * LANES))
        add_pair(k, b_all[3, part_of(k)], slice(3 * LANES, 4 * LANES))

    across = reduce_plane(1)
    near_copy(2).wait_recv()

    @pl.loop(0, CHUNKS)
    def _(k):
        add_block(5, k)

    fifth = reduce_plane(2)
    reduce_deep(0, early)
    reduce_deep(1, across)
    reduce_deep(2, fifth)

    @pl.loop(0, CHUNKS)
    def _(k):
        last_copy(k).wait_recv()
        add_block(6, k)

    sixth = reduce_plane(3)
    spread_column(0)
    spread_column(1)
    spread_column(2)
    reduce_deep(3, sixth)
    early = spread_first(0)
    across = spread_first(1)
    fifth = spread_first(2)
    spread_column(3)
    early = spread_second(0, early)
    across = spread_second(1, across)
    fifth = spread_second(2, fifth)
    sixth = spread_sheet(3)
    early = share(0, early)
    place_tiles(0, early)
    across = share(1, across)
    fifth = share(2, fifth)
    sixth = share(3, sixth)
    place_tiles(1, across)
    place_tiles(2, fifth)
    place_tiles(3, sixth)

    for i in range(3):
        near_copy(i).wait_send()

    @pl.loop(0, CHUNKS)
    def _(k):
        last_copy(k).wait_send()
        b_copy(0, k).wait_send()
        b_copy(1, k).wait_send()
        forward(0, k).wait_send()

    for n, batch in enumerate(BATCHES):
        for i in range(len(deep)):
            guarded(within(turned("zh", deep[i]), batch), lambda: deep_copy(n, i).wait_send())

        def body():
            for i in range(len(column)):
                column_copy(n, i).wait_send()

        guarded(within(zh, batch), body)
    for copy in started:
        copy.wait_send()


def project(g, b, eig):
    rows, feats = g.shape
    hbm = pl.BlockSpec(memory_space=pltpu.HBM)
    vmem = pl.BlockSpec(memory_space=pltpu.VMEM)
    dma = pltpu.SemaphoreType.DMA
    f32, bf16 = jnp.float32, jnp.bfloat16
    count = len(BATCHES)
    return pl.pallas_call(
        project_kernel,
        out_shape=pltpu.VMEM((2, 4, 4, 7, 8, TILE, LANES), bf16),
        in_specs=[hbm, hbm, hbm],
        out_specs=vmem,
        scratch_shapes=[
            pltpu.VMEM(eig.shape, f32),
            pltpu.VMEM((rows, feats), bf16),
            pltpu.VMEM((rows, feats), bf16),
            pltpu.VMEM((4, feats, LANES), bf16),
            pltpu.VMEM((7, 8, TILE, 4 * LANES), f32),
            pltpu.VMEM((7, 7, TILE, 4 * LANES), f32),
            pltpu.VMEM((4, 7, TILE, LANES), f32),
            pltpu.VMEM((3, 7, TILE, LANES), f32),
            *(
                pltpu.VMEM((4, 8, 2, high - low, last - first, TILE, LANES), bf16)
                for first, last, low, high in BATCHES
            ),
            pltpu.SemaphoreType.REGULAR((ROUNDS,)),
            dma((3,)),
            dma((3 + CHUNKS,)), dma((3 + CHUNKS,)),
            dma((2, CHUNKS)), dma((2, CHUNKS)),
            dma((CHUNKS,)), dma((CHUNKS,)),
            dma((count, 7)), dma((count, 7)),
            dma((count, 3)), dma((count, 3)),
            dma((count, 7)), dma((count, 7)),
            dma((count, 15)), dma((count, 15)),
            dma((count,)), dma((count,)),
        ],
        compiler_params=pltpu.CompilerParams(
            collective_id=0, has_side_effects=True, vmem_limit_bytes=40 << 20
        ),
    )(*(pltpu.with_memory_space_constraint(a, pltpu.HBM) for a in (g, b, eig)))


HALF = 224
STEPS = 2


def score_kernel(first, w, store, index, out):
    columns = out.shape[1]
    here = first[0] + lax.broadcasted_iota(jnp.int32, (HALF, LANES), 1)

    def wide(half, x):
        pieces = []
        for q in range(2):
            start = (half if q == 0 else 1 - half) * HALF
            for c in range(4):
                p = [t % 4 for t in TURNS].index((c - x) % 4)
                pieces.append(w[q, p, x, start : start + HALF])
        return jnp.concatenate(pieces, axis=1)

    def wanted(block):
        lines, stop = [], (block + 1) * HALF
        row = block * HALF
        while row < stop:
            tile = row // LANES * LANES
            end = min(stop, tile + LANES)
            line = index[tile : tile + LANES].reshape(1, LANES)
            lines.append(jnp.broadcast_to(line, (LANES, LANES)).T[row - tile : end - tile])
            row = end
        return jnp.concatenate(lines, axis=0)

    for step in range(STEPS):

        @pl.when(pl.program_id(0) == step)
        def _():
            for i in range(8 // STEPS):
                block = step * (8 // STEPS) + i
                product = lax.dot_general(
                    wide(block // 4, block % 4), store[...], (((1,), (1,)), ((), ())),
                    preferred_element_type=jnp.float32,
                )
                hit = wanted(block) - here
                lines = slice(i * HALF, (i + 1) * HALF)
                for n in range(0, columns, LANES):
                    lanes = slice(n, n + LANES)
                    out[lines, lanes] = jnp.where(hit == n, 0.0, product[:, lanes])


def score(first, w, store, index):
    columns, depth = store.shape
    count = index.shape[0]
    vmem = pl.BlockSpec(memory_space=pltpu.VMEM)
    return pl.pallas_call(
        score_kernel,
        out_shape=jax.ShapeDtypeStruct((count, columns), jnp.float32),
        grid=(STEPS,),
        in_specs=[pl.BlockSpec(memory_space=pltpu.SMEM), vmem, vmem, vmem],
        out_specs=pl.BlockSpec((count // STEPS, columns), lambda i: (i, 0)),
        compiler_params=pltpu.CompilerParams(vmem_limit_bytes=24 << 20),
    )(first, w, store, index)


def shards(slab_grads, basis, eigenvalues, store_rows, slab_index):
    zl, x, y, zh, core = (lax.axis_index(a) for a in AXES)
    place = (((zl * 4 + x) * 4 + y) * 4 + zh) * 2 + core
    first = (place * store_rows.shape[0]).astype(jnp.int32).reshape(1)
    w = project(slab_grads, basis, eigenvalues.reshape(8, LANES))
    w = w.reshape(2, 4, 4, 7 * BLOCK, LANES)
    return score(first, w, store_rows, slab_index)


def solution(mesh):
    split = Mesh(mesh.devices.reshape(2, 4, 4, 4, 2), AXES)
    rows, feat = ("zl", "x"), ("y", "zh", "core")
    placed = (P(rows, feat), P(feat, rows), P(), P(rows + feat, None), P())
    return jax.shard_map(
        shards, mesh=split, in_specs=placed, out_specs=P(None, rows + feat), check_vma=False
    )
```
